32 devices in a mesh: groups: 2 (over x), seq: 16 (over z, y, core).
Axes of the slice: x: 2, y: 2, z: 4, core: 2. Of those that a mesh axis runs over, the one named last changes fastest.
Arguments:
- enc_input: bfloat16 [8192, 1408], P(('groups', 'seq')), parts along dimension 0, may hold values from -6 to 6
- enc_weight: bfloat16 [2816, 1536], P('seq'), may hold values from -0.109375 to 0.109375
- norm_gain: float32 [1536], replicated, may hold values from 0.5 to 1.5
- q_weight: bfloat16 [1536, 1024], replicated, may hold values from -1 to 1
- kv_weight: bfloat16 [1536, 320], replicated, may hold values from -1 to 1
- out_weight: bfloat16 [1536, 1536], replicated, may hold values from -0.15625 to 0.15625
- dec_weight: float32 [3, 1536], replicated, may hold values from -3 to 3
- track_weight: bfloat16 [192, 1536], P('seq'), may hold values from -0.15625 to 0.15625
- track_grad: bfloat16 [4096, 192], P('groups', 'seq'), parts along dimension 0, may hold values from -6 to 6
- track_index: int32 [384], P('groups'), parts along dimension 0, may hold values from 0 to 191, each once
- track_mask: int32 [384], P('groups'), parts along dimension 0, may hold values 0 or 1
Outputs:
- trunk_out: bfloat16 [4096, 1536], P(('groups', 'seq')), parts along dimension 0
- skip_grad: bfloat16 [4096, 1536], P(('groups', 'seq')), parts along dimension 0
- dec_weight_grad: float32 [6, 1536], P('groups'), parts along dimension 0
The draws below stay inside these ranges and needn't reach their ends.
There are 2 independent parts, one for each index of `groups`. The reference program is written for one: setup_inputs(seed, part) draws one part's arguments, and reference() takes and returns one part's arrays. A program takes and returns all parts, laid end to end along the dimension named above; an argument that names none is the same for every part. Nothing has to cross between parts.
Inputs may be any that keep to these rules, and one draw needn't show every extreme that they name: `track_index`: names every track once.
All inputs are finite; a program needn't handle non-finite values.
Results may differ from the reference program's by a relative error of at most 0.02.
Values may be sent and summed in bfloat16 or wider, within the bound.
No kernel may reach another device: no remote copies, remote signals or barrier semaphores. Data moves between devices by JAX's collectives and lax.ppermute only.
A program may use at most 128 MiB of HBM per device.

```python
import jax
import jax.numpy as jnp
from jax import lax

C_IN = 1408
D = 1536
HEADS = 8
QK = 128
VDIM = 192
DILATION_SPAN = 8
TOKEN_COUNT = 2048
TRACKS = 192


def draw_q_weight(key, part):
    unit_scale = 1.0 / jnp.sqrt(jnp.float32(D))
    random_part = jnp.clip(jax.random.normal(jax.random.fold_in(key, 1), (D, HEADS * QK), jnp.float32), -6.0, 6.0) * unit_scale
    return jnp.clip(random_part, -1.0, 1.0).astype(jnp.bfloat16)


def draw_kv_weight(key, part):
    unit_scale = 1.0 / jnp.sqrt(jnp.float32(D))
    random_part = jnp.clip(jax.random.normal(jax.random.fold_in(key, 2), (D, QK + VDIM), jnp.float32), -6.0, 6.0) * unit_scale
    return jnp.clip(random_part, -1.0, 1.0).astype(jnp.bfloat16)


def set_ends(values, own_key, smallest, largest):
    spot = [jax.random.randint(jax.random.fold_in(own_key, axis), (), 0, length) for axis, length in enumerate(values.shape)]
    widest = values.shape.index(max(values.shape))
    neighbour = spot[:widest] + [(spot[widest] + 1) % values.shape[widest]] + spot[widest + 1:]
    return values.at[tuple(spot)].set(smallest).at[tuple(neighbour)].set(largest)


def steps_of(own_key, dims, cuts, smallest, largest):
    gain, own = 1.0, jax.random.fold_in(own_key, 6)
    for axis_at, blocks in cuts:
        draws = jnp.exp(jax.random.uniform(jax.random.fold_in(own, axis_at), (blocks,), jnp.float32, smallest / len(cuts), largest / len(cuts)))
        gain = gain * jnp.repeat(draws, dims[axis_at] // blocks).reshape([-1 if axis == axis_at else 1 for axis in range(len(dims))])
    return gain


def normal_values(rng, dims, spread, bound, cuts=(), kind=jnp.bfloat16):
    array = spread * jax.random.normal(rng, dims, jnp.float32)
    if cuts:
        array = array * steps_of(rng, dims, cuts, -0.22, 0.18)
    return jnp.clip(array, -bound, bound).astype(kind)


def setup_inputs(seed: int = 0, part: int = 0) -> dict:
    splits = jax.random.split(jax.random.key(seed), 12)
    own_keys = jax.random.split(jax.random.fold_in(splits[11], part), 12)
    enc_input = normal_values(own_keys[0], (2 * TOKEN_COUNT, C_IN), 1.0, 6.0, ((0, 16),))
    enc_weight = normal_values(splits[1], (2 * C_IN, D), (2 * C_IN) ** -0.5, 0.109375, ((0, 16),))
    norm_gain = jnp.clip(1.0 + 0.1 * jax.random.normal(splits[2], (D,), jnp.float32), 0.5, 1.5)
    q_weight = draw_q_weight(jax.random.fold_in(splits[11], 71), part)
    kv_weight = draw_kv_weight(jax.random.fold_in(splits[11], 71), part)
    out_weight = normal_values(splits[5], (HEADS * VDIM, D), (HEADS * VDIM) ** -0.5, 0.15625)
    dec_weight = normal_values(splits[6], (3, D), 0.5, 3.0, (), jnp.float32)
    track_weight = normal_values(splits[7], (TRACKS, D), D ** -0.5, 0.15625, ((0, 16),))
    track_grad = normal_values(own_keys[8], (TOKEN_COUNT, TRACKS), 1.0, 6.0, ((1, 16),))
    track_index = jax.random.permutation(own_keys[9], TRACKS).astype(jnp.int32)
    track_mask = set_ends((jax.random.randint(own_keys[10], (TRACKS,), 0, 4) < 3).astype(jnp.int32), jax.random.fold_in(own_keys[10], 1), 0, 1)
    return {"enc_input": enc_input, "enc_weight": enc_weight, "norm_gain": norm_gain, "q_weight": q_weight, "kv_weight": kv_weight, "out_weight": out_weight, "dec_weight": dec_weight, "track_weight": track_weight, "track_grad": track_grad, "track_index": track_index, "track_mask": track_mask}


def gelu_tanh(values):
    return jax.nn.gelu(values, approximate=True)

def reference(enc_input, enc_weight, norm_gain, q_weight, kv_weight, out_weight, dec_weight, track_weight, track_grad, track_index, track_mask):
    patches = enc_input.reshape(TOKEN_COUNT, 2 * C_IN)
    tokens = jnp.dot(patches, enc_weight, preferred_element_type=jnp.float32).astype(jnp.bfloat16)
    tok_f = tokens.astype(jnp.float32)
    normed = (tok_f * lax.rsqrt(lax.optimization_barrier(jnp.mean(tok_f * tok_f, axis=-1, keepdims=True)) + 1e-06) * norm_gain).astype(jnp.bfloat16)
    query = jnp.dot(normed, q_weight, preferred_element_type=jnp.float32).astype(jnp.bfloat16)
    keyval = jnp.dot(normed, kv_weight, preferred_element_type=jnp.float32).astype(jnp.bfloat16)
    keys = keyval[:, :QK]
    values = keyval[:, QK:]
    block = 256 if TOKEN_COUNT % 256 == 0 else TOKEN_COUNT

    def attend(query_block):
        rows = query_block.reshape(block * HEADS, QK)
        scores = lax.dot_general(rows, keys, (((1,), (1,)), ((), ())), preferred_element_type=jnp.float32) * QK ** (-0.5)
        top = lax.optimization_barrier(jnp.max(scores, axis=1, keepdims=True))
        expw = jnp.exp(scores - top)
        total = lax.optimization_barrier(jnp.sum(expw, axis=1, keepdims=True))
        weighted = jnp.dot(expw.astype(jnp.bfloat16), values, preferred_element_type=jnp.float32)
        return (weighted / total).reshape(block, HEADS * VDIM).astype(jnp.bfloat16)
    context = lax.map(attend, query.reshape(TOKEN_COUNT // block, block, HEADS * QK)).reshape(TOKEN_COUNT, HEADS * VDIM)
    trunk_out = (tok_f + jnp.dot(context, out_weight, preferred_element_type=jnp.float32)).astype(jnp.bfloat16)
    masked = track_grad * track_mask.astype(jnp.bfloat16)[None, :]
    selected = jnp.take(track_weight, track_index, axis=0)
    head_gradient = jnp.dot(masked, selected, preferred_element_type=jnp.float32).astype(jnp.bfloat16)
    padded_input = jnp.pad(head_gradient.astype(jnp.float32), ((DILATION_SPAN, DILATION_SPAN), (0, 0)))
    skip_act, pullback = jax.vjp(gelu_tanh, tok_f)
    convback = jnp.zeros((TOKEN_COUNT, D), jnp.float32)
    tap_terms = []
    for shift_amount in range(3):
        shifted_rows = padded_input[DILATION_SPAN * (2 - shift_amount):DILATION_SPAN * (2 - shift_amount) + TOKEN_COUNT]
        convback = convback + dec_weight[shift_amount][None, :] * shifted_rows
        tap_terms.append(lax.optimization_barrier(jnp.sum(skip_act * shifted_rows, axis=0)))
    skip_grad = pullback(convback)[0].astype(jnp.bfloat16)
    dec_weight_grad = jnp.stack(tap_terms, axis=0) / jnp.sqrt(jnp.float32(TOKEN_COUNT))
    return (trunk_out, skip_grad, dec_weight_grad)
```

```python
import functools
import math

import jax
import jax.numpy as jnp
from jax import lax
from jax.experimental import pallas as pl
from jax.experimental.pallas import tpu as pltpu
from jax.sharding import Mesh, PartitionSpec as P

HEADS = 8
QK = 128
VDIM = 192
SPAN = 8
MIB = 1 << 20
VMEM = pl.BlockSpec(memory_space=pltpu.VMEM)
SMEM = pl.BlockSpec(memory_space=pltpu.SMEM)
ANY = pl.BlockSpec(memory_space=pl.ANY)


def chip_swap(cells, mask):
    count = lax.axis_size("chip")
    return lax.ppermute(cells, "chip", [(i, i ^ mask) for i in range(count)])


def core_swap(cells):
    return lax.ppermute(cells, "core", [(0, 1), (1, 0)])


def group_swap(cells):
    return lax.ppermute(cells, "groups", [(0, 1), (1, 0)])


def after(value, *others):
    return lax.optimization_barrier((value, *others))[0]


def tokens_kernel(rows, extra, ids_ref, own_ref, partner_ref, *refs):
    blocks, (own_out, partner_out, tracks_out, x_s, w_s, sems) = refs[:-6], refs[-6:]
    copies = []
    for at, block in enumerate(blocks):
        spot = ids_ref[at]
        for which, (first, length, target) in enumerate(
            ((0, rows, w_s), (rows, extra, tracks_out))
        ):
            copy = pltpu.make_async_copy(
                block.at[pl.ds(first, length)],
                target.at[pl.ds(pl.multiple_of(spot * length, 8), length)],
                sems.at[at, which],
            )
            copy.start()
            copies.append(copy)
    pairs, width = own_ref.shape
    half = pairs // 2
    line = lax.broadcasted_iota(jnp.int32, (half, pairs), 0)
    column = lax.broadcasted_iota(jnp.int32, (half, pairs), 1)
    for tap in range(2):
        pick = (column == 2 * line + tap).astype(jnp.bfloat16)
        for part, ref in enumerate((own_ref, partner_ref)):
            x_s[part * half : (part + 1) * half, tap * width : (tap + 1) * width] = jnp.dot(
                pick, ref[...], preferred_element_type=jnp.float32
            ).astype(jnp.bfloat16)
    for copy in copies:
        copy.wait()
    total = jnp.dot(x_s[...], w_s[...], preferred_element_type=jnp.float32).astype(jnp.bfloat16)
    own_out[...] = total[:half]
    partner_out[...] = total[half:]


def windows_kernel(grad_ref, out_ref):
    tracks = grad_ref.shape[0]
    count, lines, lanes = out_ref.shape
    rows = grad_ref.shape[1] // count
    lane = lax.broadcasted_iota(jnp.int32, (tracks, rows), 1)
    zero = jnp.zeros((tracks, rows), jnp.float32)
    out_ref[...] = jnp.zeros_like(out_ref)
    tiles = [grad_ref[:, at * rows : (at + 1) * rows].astype(jnp.float32) for at in range(count)]
    for at in range(count):
        after_it = tiles[at + 1] if at + 1 < count else zero
        before_it = pltpu.roll(tiles[at - 1], 2 * SPAN, 1) if at else zero
        edge = jnp.where(lane < SPAN, after_it, jnp.where(lane < 2 * SPAN, before_it, zero))
        out_ref[at, 0:tracks, 0:rows] = tiles[at].astype(out_ref.dtype)
        out_ref[at, 0:tracks, rows : 2 * rows] = edge.astype(out_ref.dtype)


def keyval_kernel(group_ref, mine_ref, theirs_ref, gain_ref, kv_ref, tok_ref, normed_ref, keyval_ref):
    width = mine_ref.shape[1]
    group = group_ref[0]
    tok_ref[:, pl.ds(pl.multiple_of(group * width, width), width)] = mine_ref[...]
    tok_ref[:, pl.ds(pl.multiple_of((1 - group) * width, width), width)] = theirs_ref[...]
    tok_f = tok_ref[...].astype(jnp.float32)
    inverse = lax.rsqrt(jnp.mean(tok_f * tok_f, axis=-1, keepdims=True) + 1e-06)
    normed = (tok_f * inverse * gain_ref[...]).astype(jnp.bfloat16)
    normed_ref[...] = normed
    keyval_ref[...] = lax.dot_general(
        normed, kv_ref[...], (((1,), (1,)), ((), ())), preferred_element_type=jnp.float32
    ).astype(jnp.bfloat16)


def sweep(turns, step, body, carry):
    if turns <= 4:
        for turn in range(turns):
            carry = body(turn * step, carry)
        return carry
    return lax.fori_loop(
        0, turns, lambda turn, held: body(pl.multiple_of(turn * step, step), held), carry
    )


def query_kernel(normed_ref, weight_ref, out_ref):
    rows = normed_ref.shape[0]
    query = jnp.dot(normed_ref[...], weight_ref[...], preferred_element_type=jnp.float32).astype(
        jnp.bfloat16
    )
    for h in range(HEADS):
        out_ref[h * rows : (h + 1) * rows, :] = query[:, h * QK : (h + 1) * QK]


def attention_kernel(row_block, key_block, pieces, first, last, query_ref, *refs):
    kv_refs, refs = refs[:pieces], refs[pieces:]
    if not first:
        old_top_ref, old_weighted_ref = refs[:2]
        refs = refs[2:]
    if last:
        tok_ref, outw_ref, out_ref, k_s, v_s, s_s = refs
        token_rows = tok_ref.shape[0]
        total = tok_ref[...].astype(jnp.float32)
    else:
        top_ref, weighted_ref, k_s, v_s, s_s = refs
    at = 0
    for ref in kv_refs:
        count = ref.shape[0]
        k_s[at : at + count, :] = ref[:, :QK]
        v_s[at : at + count, 0:VDIM] = ref[:, QK:]
        at += count
    key_block = min(key_block, at)
    v_s[:, VDIM:] = jnp.ones((at, v_s.shape[1] - VDIM), jnp.bfloat16)
    scale = QK ** (-0.5) / math.log(2.0)
    for r in range(0, query_ref.shape[0], row_block):
        rows = query_ref[r : r + row_block, :]
        slot = (r // row_block) % 2

        def score(k, top):
            scores = lax.dot_general(
                rows,
                k_s[pl.ds(k, key_block), :],
                (((1,), (1,)), ((), ())),
                preferred_element_type=jnp.float32,
            )
            s_s[slot, :, pl.ds(k, key_block)] = scores
            return jnp.maximum(top, jnp.max(scores, axis=1, keepdims=True))

        def weigh(k, weighted):
            shifted = s_s[slot, :, pl.ds(k, key_block)] - top
            expw = jnp.exp2(shifted * scale).astype(jnp.bfloat16)
            return weighted + jnp.dot(
                expw, v_s[pl.ds(k, key_block), :], preferred_element_type=jnp.float32
            )

        if first:
            old_top = jnp.full((row_block, 1), -jnp.inf, jnp.float32)
            start = jnp.zeros((row_block, v_s.shape[1]), jnp.float32)
        else:
            old_top = old_top_ref[r : r + row_block, 0:1]
        top = sweep(at // key_block, key_block, score, old_top)
        if not first:
            start = old_weighted_ref[r : r + row_block, :] * jnp.exp2((old_top - top) * scale)
        weighted = sweep(at // key_block, key_block, weigh, start)
        if last:
            context = (weighted[:, :VDIM] / weighted[:, VDIM : VDIM + 1]).astype(jnp.bfloat16)
            for j in range(row_block // token_rows):
                h = r // token_rows + j
                total = total + jnp.dot(
                    context[j * token_rows : (j + 1) * token_rows],
                    outw_ref[h * VDIM : (h + 1) * VDIM, :],
                    preferred_element_type=jnp.float32,
                )
        else:
            top_ref[r : r + row_block, :] = jnp.broadcast_to(top, (row_block, top_ref.shape[1]))
            weighted_ref[r : r + row_block, :] = weighted
    if last:
        out_ref[...] = total.astype(jnp.bfloat16)


def decoder_kernel(extra, tok_ref, grads_ref, chosen_ref, tracks_ref, taps_ref, skip_ref, sums_ref):
    token_rows = tok_ref.shape[0]
    width = tracks_ref.shape[1]
    root = math.sqrt(2.0 / math.pi)
    masked = lax.dot_general(
        grads_ref[...],
        chosen_ref[...],
        (((0,), (0,)), ((), ())),
        preferred_element_type=jnp.float32,
    )[: token_rows + 2 * SPAN]
    column = lax.broadcasted_iota(jnp.int32, masked.shape, 1) % extra
    for side in range(2):
        at = side * width
        ours = (column < extra // 2) if side == 0 else (column >= extra // 2)
        rows = jnp.where(ours, masked, 0.0).astype(jnp.bfloat16)
        head = (
            jnp.dot(rows, tracks_ref[...], preferred_element_type=jnp.float32)
            .astype(jnp.bfloat16)
            .astype(jnp.float32)
        )
        own, later, earlier = (
            head[:token_rows],
            head[token_rows : token_rows + SPAN],
            head[token_rows + SPAN :],
        )
        shifted_rows = (
            jnp.concatenate([own[SPAN:], later], axis=0),
            own,
            jnp.concatenate([earlier, own[:-SPAN]], axis=0),
        )
        tok = tok_ref[:, at : at + width].astype(jnp.float32)
        square = tok * tok
        curve = jnp.tanh(root * (tok + 0.044715 * square * tok))
        gate = 0.5 * (1.0 + curve)
        act = tok * gate
        slope = gate + 0.5 * tok * (1.0 - curve * curve) * (root * (1.0 + 3 * 0.044715 * square))
        convback = jnp.zeros_like(tok)
        for tap, shifted in enumerate(shifted_rows):
            convback = convback + taps_ref[tap : tap + 1, at : at + width] * shifted
            sums_ref[tap : tap + 1, at : at + width] = jnp.sum(act * shifted, axis=0, keepdims=True)
        skip_ref[:, at : at + width] = (slope * convback).astype(jnp.bfloat16)


def call(body, out, specs, scratch=(), limit=32, name=None):
    return pl.pallas_call(
        body,
        out_shape=out,
        in_specs=specs,
        out_specs=jax.tree.map(lambda _: VMEM, out),
        scratch_shapes=list(scratch),
        compiler_params=pltpu.CompilerParams(vmem_limit_bytes=limit * MIB),
        name=name,
    )


def shards(
    enc_input,
    enc_weight,
    norm_gain,
    q_weight,
    kv_weight,
    out_weight,
    dec_weight,
    track_weight,
    track_grad,
    track_index,
    track_mask,
):
    chips = lax.axis_size("chip")
    count = 2 * chips
    pair = chips // 2
    token_rows = enc_input.shape[0] // 2
    rows, dim = enc_weight.shape
    width = dim // 2
    tracks = track_weight.shape[0]
    extra = 2 * tracks
    group = lax.axis_index("groups")
    me = lax.axis_index("chip") * 2 + lax.axis_index("core")
    shape = lambda *dims, kind=jnp.bfloat16: jax.ShapeDtypeStruct(dims, kind)
    direct = pair <= 4 and pair & (pair - 1) == 0 and rows % 16 == 0

    own_half = lax.dynamic_slice_in_dim(enc_weight, group * width, width, axis=1)
    packed = jnp.concatenate([own_half, track_weight[:, :width], track_weight[:, width:]], axis=0)
    if direct:
        lanes = {0: packed}
        for mask in range(1, pair):
            lanes[mask] = chip_swap(after(packed, lanes[1]) if mask == 3 else packed, 2 * mask)
        grads = after(track_grad, lanes[1]) if pair > 1 else track_grad
    else:
        grads = track_grad
    partner_input = group_swap(enc_input)

    lines = -(-tracks // 16) * 16
    windows = call(windows_kernel, shape(count, lines, 2 * token_rows), [VMEM], name="windows")(
        grads.T
    )
    exchanged = lax.all_to_all(windows, ("chip", "core"), 0, 0, tiled=True)
    slots = jnp.pad(
        track_index.reshape(count, tracks), ((0, 0), (0, lines - tracks)), constant_values=-1
    )
    measured = jnp.pad(track_mask.reshape(count, tracks), ((0, 0), (0, lines - tracks)))
    columns = jnp.arange(count * extra, dtype=jnp.int32)
    column_tracks = columns // extra * tracks + columns % tracks
    chosen = jnp.where(
        slots.reshape(-1, 1) == column_tracks[None, :],
        measured.reshape(-1, 1).astype(jnp.bfloat16),
        0,
    ).astype(jnp.bfloat16)

    if direct:
        blocks = []
        for mask in range(pair):
            near = lanes[mask]
            far = chip_swap(after(near, exchanged) if mask == 2 else near, 1)
            blocks += [
                (4 * mask, near),
                (4 * mask + 1, core_swap(near)),
                (4 * mask + 2, far),
                (4 * mask + 3, core_swap(far)),
            ]
        ids = me ^ jnp.array([mask for mask, _ in blocks], jnp.int32)
        mine, partner, track_rows = call(
            functools.partial(tokens_kernel, rows, extra),
            (
                shape(token_rows, width),
                shape(token_rows, width),
                shape(count * extra, width),
            ),
            [SMEM, VMEM, VMEM] + [ANY] * count,
            scratch=(
                pltpu.VMEM((2 * token_rows, count * rows), jnp.bfloat16),
                pltpu.VMEM((count * rows, width), jnp.bfloat16),
                pltpu.SemaphoreType.DMA((count, 2)),
            ),
            name="tokens",
        )(ids, enc_input, partner_input, *[block for _, block in blocks])
    else:
        gathered = lax.all_gather(packed, ("chip", "core"), axis=0)
        track_rows = gathered[:, rows:].reshape(count * extra, width)
        weight = gathered[:, :rows].reshape(count * rows, width)
        mine, partner = (
            jnp.dot(
                cells.reshape(token_rows, count * rows), weight, preferred_element_type=jnp.float32
            ).astype(jnp.bfloat16)
            for cells in (enc_input, partner_input)
        )
    theirs = group_swap(partner)
    tokens, normed, keyval = call(
        keyval_kernel,
        (shape(token_rows, dim), shape(token_rows, dim), shape(token_rows, QK + VDIM)),
        [SMEM] + [VMEM] * 4,
        name="keyval",
    )(group.reshape(1), mine, theirs, norm_gain.reshape(1, dim), kv_weight.T)

    if direct:
        early, late = [], []
        for mask in range(pair):
            near = chip_swap(keyval, 2 * mask) if mask else keyval
            far = chip_swap(near, 1)
            side = early if mask < max(1, pair // 2) else late
            side += [near, far, core_swap(near), core_swap(far)]
        stages = [side for side in (early, late) if side]
    else:
        stages = [[lax.all_gather(keyval, ("chip", "core"), axis=0, tiled=True)]]

    query = call(query_kernel, shape(HEADS * token_rows, QK), [VMEM] * 2, name="query")(
        normed, q_weight
    )
    skip_grad, sums = call(
        functools.partial(decoder_kernel, extra),
        (shape(token_rows, dim), shape(3, dim, kind=jnp.float32)),
        [VMEM] * 5,
        name="decoder",
    )(tokens, exchanged.reshape(count * lines, 2 * token_rows), chosen, track_rows, dec_weight)
    sums = sums + core_swap(sums)
    step = 1
    while step < chips:
        sums = sums + chip_swap(sums, step)
        step *= 2
    dec_weight_grad = sums / jnp.float32(math.sqrt(token_rows * count))

    row_block = 2 * token_rows if direct else token_rows
    state = []
    for turn, pieces in enumerate(stages):
        last = turn + 1 == len(stages)
        keys = sum(piece.shape[0] for piece in pieces)
        extras = [tokens, out_weight] if last else []
        held = (
            shape(token_rows, dim)
            if last
            else (
                shape(HEADS * token_rows, 128, kind=jnp.float32),
                shape(HEADS * token_rows, 256, kind=jnp.float32),
            )
        )
        state = call(
            functools.partial(attention_kernel, row_block, 512, len(pieces), turn == 0, last),
            held,
            [VMEM] * (1 + len(pieces) + len(state) + len(extras)),
            scratch=(
                pltpu.VMEM((keys, QK), jnp.bfloat16),
                pltpu.VMEM((keys, 256), jnp.bfloat16),
                pltpu.VMEM((2, row_block, keys), jnp.float32),
            ),
            limit=60 if len(stages) == 1 else 40,
            name="attention",
        )(query, *pieces, *state, *extras)
    return (state, skip_grad, dec_weight_grad)


def solution(mesh):
    groups, count = mesh.devices.shape
    inner = Mesh(mesh.devices.reshape(groups, count // 2, 2), ("groups", "chip", "core"))
    seq = ("chip", "core")
    every = ("groups", "chip", "core")
    return jax.shard_map(
        shards,
        mesh=inner,
        in_specs=(
            P(every, None),
            P(seq, None),
            P(),
            P(),
            P(),
            P(),
            P(),
            P(seq, None),
            P("groups", seq),
            P("groups"),
            P("groups"),
        ),
        out_specs=(P(every, None), P(every, None), P("groups", None)),
        check_vma=False,
    )
```

```python
import functools
import math

import jax
import jax.numpy as jnp
from jax import lax
from jax.experimental import pallas as pl
from jax.experimental.pallas import tpu as pltpu
from jax.sharding import Mesh, PartitionSpec as P

HEADS = 8
QK = 128
VDIM = 192
SPAN = 8
MIB = 1 << 20
VMEM = pl.BlockSpec(memory_space=pltpu.VMEM)
SMEM = pl.BlockSpec(memory_space=pltpu.SMEM)
HBM = pl.BlockSpec(memory_space=pltpu.HBM)


def chip_swap(cells, mask):
    count = lax.axis_size("chip")
    return lax.ppermute(cells, "chip", [(i, i ^ mask) for i in range(count)])


def core_swap(cells):
    return lax.ppermute(cells, "core", [(0, 1), (1, 0)])


def group_swap(cells):
    return lax.ppermute(cells, "groups", [(0, 1), (1, 0)])


def after(value, *others):
    return lax.optimization_barrier((value, *others))[0]


def tokens_kernel(rows, extra, ids_ref, own_ref, partner_ref, *refs):
    blocks, (own_out, partner_out, tracks_out, x_s, w_s, sems) = refs[:-6], refs[-6:]
    copies = []
    for at, block in enumerate(blocks):
        spot = ids_ref[at]
        for which, (first, length, target) in enumerate(
            ((0, rows, w_s), (rows, extra, tracks_out))
        ):
            copy = pltpu.make_async_copy(
                block.at[pl.ds(first, length)],
                target.at[pl.ds(pl.multiple_of(spot * length, 8), length)],
                sems.at[at, which],
            )
            copy.start()
            copies.append(copy)
    pairs, width = own_ref.shape
    half = pairs // 2
    line = lax.broadcasted_iota(jnp.int32, (half, pairs), 0)
    column = lax.broadcasted_iota(jnp.int32, (half, pairs), 1)
    for tap in range(2):
        pick = (column == 2 * line + tap).astype(jnp.bfloat16)
        for part, ref in enumerate((own_ref, partner_ref)):
            x_s[part * half : (part + 1) * half, tap * width : (tap + 1) * width] = jnp.dot(
                pick, ref[...], preferred_element_type=jnp.float32
            ).astype(jnp.bfloat16)
    for copy in copies:
        copy.wait()
    total = jnp.dot(x_s[...], w_s[...], preferred_element_type=jnp.float32).astype(jnp.bfloat16)
    own_out[...] = total[:half]
    partner_out[...] = total[half:]


def windows_kernel(grad_ref, out_ref):
    tracks = grad_ref.shape[0]
    count, lines, lanes = out_ref.shape
    rows = grad_ref.shape[1] // count
    lane = lax.broadcasted_iota(jnp.int32, (tracks, rows), 1)
    zero = jnp.zeros((tracks, rows), jnp.float32)
    out_ref[...] = jnp.zeros_like(out_ref)
    tiles = [grad_ref[:, at * rows : (at + 1) * rows].astype(jnp.float32) for at in range(count)]
    for at in range(count):
        after_it = tiles[at + 1] if at + 1 < count else zero
        before_it = pltpu.roll(tiles[at - 1], 2 * SPAN, 1) if at else zero
        edge = jnp.where(lane < SPAN, after_it, jnp.where(lane < 2 * SPAN, before_it, zero))
        out_ref[at, 0:tracks, 0:rows] = tiles[at].astype(out_ref.dtype)
        out_ref[at, 0:tracks, rows : 2 * rows] = edge.astype(out_ref.dtype)


def keyval_kernel(group_ref, mine_ref, theirs_ref, gain_ref, kv_ref, tok_ref, normed_ref, keyval_ref):
    width = mine_ref.shape[1]
    group = group_ref[0]
    tok_ref[:, pl.ds(pl.multiple_of(group * width, width), width)] = mine_ref[...]
    tok_ref[:, pl.ds(pl.multiple_of((1 - group) * width, width), width)] = theirs_ref[...]
    tok_f = tok_ref[...].astype(jnp.float32)
    inverse = lax.rsqrt(jnp.mean(tok_f * tok_f, axis=-1, keepdims=True) + 1e-06)
    normed = (tok_f * inverse * gain_ref[...]).astype(jnp.bfloat16)
    normed_ref[...] = normed
    keyval_ref[...] = lax.dot_general(
        normed, kv_ref[...], (((1,), (1,)), ((), ())), preferred_element_type=jnp.float32
    ).astype(jnp.bfloat16)


def sweep(turns, step, body, carry):
    if turns <= 4:
        for turn in range(turns):
            carry = body(turn * step, carry)
        return carry
    return lax.fori_loop(
        0, turns, lambda turn, held: body(pl.multiple_of(turn * step, step), held), carry
    )


def query_kernel(normed_ref, weight_ref, out_ref):
    rows = normed_ref.shape[0]
    query = jnp.dot(normed_ref[...], weight_ref[...], preferred_element_type=jnp.float32).astype(
        jnp.bfloat16
    )
    for h in range(HEADS):
        out_ref[h * rows : (h + 1) * rows, :] = query[:, h * QK : (h + 1) * QK]


def attention_kernel(row_block, key_block, pieces, first, last, query_ref, *refs):
    kv_refs, refs = refs[:pieces], refs[pieces:]
    if not first:
        old_top_ref, old_weighted_ref = refs[:2]
        refs = refs[2:]
    if last:
        tok_ref, outw_ref, out_ref, k_s, v_s, s_s = refs
        token_rows = tok_ref.shape[0]
        total = tok_ref[...].astype(jnp.float32)
    else:
        top_ref, weighted_ref, k_s, v_s, s_s = refs
    at = 0
    for ref in kv_refs:
        count = ref.shape[0]
        k_s[at : at + count, :] = ref[:, :QK]
        v_s[at : at + count, 0:VDIM] = ref[:, QK:]
        at += count
    key_block = min(key_block, at)
    v_s[:, VDIM:] = jnp.ones((at, v_s.shape[1] - VDIM), jnp.bfloat16)
    scale = QK ** (-0.5) / math.log(2.0)
    for r in range(0, query_ref.shape[0], row_block):
        rows = query_ref[r : r + row_block, :]
        slot = (r // row_block) % 2

        def score(k, top):
            scores = lax.dot_general(
                rows,
                k_s[pl.ds(k, key_block), :],
                (((1,), (1,)), ((), ())),
                preferred_element_type=jnp.float32,
            )
            s_s[slot, :, pl.ds(k, key_block)] = scores
            return jnp.maximum(top, jnp.max(scores, axis=1, keepdims=True))

        def weigh(k, weighted):
            shifted = s_s[slot, :, pl.ds(k, key_block)] - top
            expw = jnp.exp2(shifted * scale).astype(jnp.bfloat16)
            return weighted + jnp.dot(
                expw, v_s[pl.ds(k, key_block), :], preferred_element_type=jnp.float32
            )

        if first:
            old_top = jnp.full((row_block, 1), -jnp.inf, jnp.float32)
            start = jnp.zeros((row_block, v_s.shape[1]), jnp.float32)
        else:
            old_top = old_top_ref[r : r + row_block, 0:1]
        top = sweep(at // key_block, key_block, score, old_top)
        if not first:
            start = old_weighted_ref[r : r + row_block, :] * jnp.exp2((old_top - top) * scale)
        weighted = sweep(at // key_block, key_block, weigh, start)
        if last:
            context = (weighted[:, :VDIM] / weighted[:, VDIM : VDIM + 1]).astype(jnp.bfloat16)
            for j in range(row_block // token_rows):
                h = r // token_rows + j
                total = total + jnp.dot(
                    context[j * token_rows : (j + 1) * token_rows],
                    outw_ref[h * VDIM : (h + 1) * VDIM, :],
                    preferred_element_type=jnp.float32,
                )
        else:
            top_ref[r : r + row_block, :] = jnp.broadcast_to(top, (row_block, top_ref.shape[1]))
            weighted_ref[r : r + row_block, :] = weighted
    if last:
        out_ref[...] = total.astype(jnp.bfloat16)


def decoder_kernel(extra, tok_ref, grads_ref, chosen_ref, tracks_ref, taps_ref, skip_ref, sums_ref):
    token_rows = tok_ref.shape[0]
    width = tracks_ref.shape[1]
    root = math.sqrt(2.0 / math.pi)
    masked = lax.dot_general(
        grads_ref[...],
        chosen_ref[...],
        (((0,), (0,)), ((), ())),
        preferred_element_type=jnp.float32,
    )[: token_rows + 2 * SPAN]
    column = lax.broadcasted_iota(jnp.int32, masked.shape, 1) % extra
    for side in range(2):
        at = side * width
        ours = (column < extra // 2) if side == 0 else (column >= extra // 2)
        rows = jnp.where(ours, masked, 0.0).astype(jnp.bfloat16)
        head = (
            jnp.dot(rows, tracks_ref[...], preferred_element_type=jnp.float32)
            .astype(jnp.bfloat16)
            .astype(jnp.float32)
        )
        own, later, earlier = (
            head[:token_rows],
            head[token_rows : token_rows + SPAN],
            head[token_rows + SPAN :],
        )
        shifted_rows = (
            jnp.concatenate([own[SPAN:], later], axis=0),
            own,
            jnp.concatenate([earlier, own[:-SPAN]], axis=0),
        )
        tok = tok_ref[:, at : at + width].astype(jnp.float32)
        square = tok * tok
        curve = jnp.tanh(root * (tok + 0.044715 * square * tok))
        gate = 0.5 * (1.0 + curve)
        act = tok * gate
        slope = gate + 0.5 * tok * (1.0 - curve * curve) * (root * (1.0 + 3 * 0.044715 * square))
        convback = jnp.zeros_like(tok)
        for tap, shifted in enumerate(shifted_rows):
            convback = convback + taps_ref[tap : tap + 1, at : at + width] * shifted
            sums_ref[tap : tap + 1, at : at + width] = jnp.sum(act * shifted, axis=0, keepdims=True)
        skip_ref[:, at : at + width] = (slope * convback).astype(jnp.bfloat16)


def call(body, out, specs, scratch=(), limit=32, name=None):
    return pl.pallas_call(
        body,
        out_shape=out,
        in_specs=specs,
        out_specs=jax.tree.map(lambda _: VMEM, out),
        scratch_shapes=list(scratch),
        compiler_params=pltpu.CompilerParams(vmem_limit_bytes=limit * MIB),
        name=name,
    )


def shards(
    enc_input,
    enc_weight,
    norm_gain,
    q_weight,
    kv_weight,
    out_weight,
    dec_weight,
    track_weight,
    track_grad,
    track_index,
    track_mask,
):
    chips = lax.axis_size("chip")
    count = 2 * chips
    pair = chips // 2
    token_rows = enc_input.shape[0] // 2
    rows, dim = enc_weight.shape
    width = dim // 2
    tracks = track_weight.shape[0]
    extra = 2 * tracks
    group = lax.axis_index("groups")
    me = lax.axis_index("chip") * 2 + lax.axis_index("core")
    shape = lambda *dims, kind=jnp.bfloat16: jax.ShapeDtypeStruct(dims, kind)
    direct = pair <= 4 and pair & (pair - 1) == 0 and rows % 16 == 0

    own_half = lax.dynamic_slice_in_dim(enc_weight, group * width, width, axis=1)
    packed = jnp.concatenate([own_half, track_weight[:, :width], track_weight[:, width:]], axis=0)
    if direct:
        lanes = {0: packed}
        for mask in range(1, pair):
            lanes[mask] = chip_swap(after(packed, lanes[1]) if mask == 3 else packed, 2 * mask)
    partner_input = group_swap(enc_input)

    lines = -(-tracks // 16) * 16
    windows = call(
        windows_kernel, shape(count, lines, 2 * token_rows), [VMEM], limit=16, name="windows"
    )(track_grad.T)
    slots = jnp.pad(
        track_index.reshape(count, tracks), ((0, 0), (0, lines - tracks)), constant_values=-1
    )
    measured = jnp.pad(track_mask.reshape(count, tracks), ((0, 0), (0, lines - tracks)))
    columns = jnp.arange(count * extra, dtype=jnp.int32)
    column_tracks = columns // extra * tracks + columns % tracks
    chosen = jnp.where(
        slots.reshape(-1, 1) == column_tracks[None, :],
        measured.reshape(-1, 1).astype(jnp.bfloat16),
        0,
    ).astype(jnp.bfloat16)

    if direct:
        blocks = []
        for mask in range(pair):
            near = lanes[mask]
            far = chip_swap(near, 1)
            blocks += [
                (4 * mask, near),
                (4 * mask + 1, core_swap(near)),
                (4 * mask + 2, far),
                (4 * mask + 3, core_swap(far)),
            ]
        ids = me ^ jnp.array([mask for mask, _ in blocks], jnp.int32)
        mine, partner, track_rows = call(
            functools.partial(tokens_kernel, rows, extra),
            (
                shape(token_rows, width),
                shape(token_rows, width),
                shape(count * extra, width),
            ),
            [SMEM, VMEM, VMEM] + [HBM] * count,
            scratch=(
                pltpu.VMEM((2 * token_rows, count * rows), jnp.bfloat16),
                pltpu.VMEM((count * rows, width), jnp.bfloat16),
                pltpu.SemaphoreType.DMA((count, 2)),
            ),
            limit=16,
            name="tokens",
        )(ids, enc_input, partner_input, *[pltpu.with_memory_space_constraint(block, pltpu.HBM) for _, block in blocks])
    else:
        gathered = lax.all_gather(packed, ("chip", "core"), axis=0)
        track_rows = gathered[:, rows:].reshape(count * extra, width)
        weight = gathered[:, :rows].reshape(count * rows, width)
        mine, partner = (
            jnp.dot(
                cells.reshape(token_rows, count * rows), weight, preferred_element_type=jnp.float32
            ).astype(jnp.bfloat16)
            for cells in (enc_input, partner_input)
        )
    theirs = group_swap(partner)
    exchanged = lax.all_to_all(after(windows, partner), ("chip", "core"), 0, 0, tiled=True)
    tokens, normed, keyval = call(
        keyval_kernel,
        (shape(token_rows, dim), shape(token_rows, dim), shape(token_rows, QK + VDIM)),
        [SMEM] + [VMEM] * 4,
        limit=8,
        name="keyval",
    )(group.reshape(1), mine, theirs, norm_gain.reshape(1, dim), kv_weight.T)

    if direct:
        nears = [chip_swap(keyval, 2 * mask) if mask else keyval for mask in range(pair)]
        fars = [chip_swap(near, 1) for near in nears]
        cut = max(1, pair // 2)
        stages = [
            [cells for piece in side for cells in (piece, core_swap(piece))]
            for side in (nears[:cut] + fars[:cut], nears[cut:] + fars[cut:])
            if side
        ]
    else:
        nears = fars = [lax.all_gather(keyval, ("chip", "core"), axis=0, tiled=True)]
        stages = [nears]

    query = call(query_kernel, shape(HEADS * token_rows, QK), [VMEM] * 2, limit=8, name="query")(
        normed, q_weight
    )
    skip_grad, sums = call(
        functools.partial(decoder_kernel, extra),
        (shape(token_rows, dim), shape(3, dim, kind=jnp.float32)),
        [VMEM] * 5,
        limit=16,
        name="decoder",
    )(after(tokens, nears[min(1, len(nears) - 1)]), exchanged.reshape(count * lines, 2 * token_rows), chosen, track_rows, dec_weight)
    row_block = 2 * token_rows if direct else token_rows
    state = []
    for turn, pieces in enumerate(stages):
        last = turn + 1 == len(stages)
        keys = sum(piece.shape[0] for piece in pieces)
        extras = [tokens, out_weight] if last else []
        held = (
            shape(token_rows, dim)
            if last
            else (
                shape(HEADS * token_rows, 128, kind=jnp.float32),
                shape(HEADS * token_rows, 256, kind=jnp.float32),
            )
        )
        state = call(
            functools.partial(attention_kernel, row_block, 512, len(pieces), turn == 0, last),
            held,
            [VMEM] * (1 + len(pieces) + len(state) + len(extras)),
            scratch=(
                pltpu.VMEM((keys, QK), jnp.bfloat16),
                pltpu.VMEM((keys, 256), jnp.bfloat16),
                pltpu.VMEM((2, row_block, keys), jnp.float32),
            ),
            limit=60 if len(stages) == 1 else 12,
            name="attention",
        )(query, *pieces, *state, *extras)
        if turn == 0:
            scored = state
    sums = sums + core_swap(sums)
    waits = [nears[-1], scored if direct else nears[-1]]
    step = 1
    while step < chips:
        held = after(sums, waits.pop(0)) if waits and len(stages) > 1 else sums
        sums = sums + chip_swap(held, step)
        step *= 2
    dec_weight_grad = sums / jnp.float32(math.sqrt(token_rows * count))
    return (state, skip_grad, dec_weight_grad)


def solution(mesh):
    groups, count = mesh.devices.shape
    inner = Mesh(mesh.devices.reshape(groups, count // 2, 2), ("groups", "chip", "core"))
    seq = ("chip", "core")
    every = ("groups", "chip", "core")
    return jax.shard_map(
        shards,
        mesh=inner,
        in_specs=(
            P(every, None),
            P(seq, None),
            P(),
            P(),
            P(),
            P(),
            P(),
            P(seq, None),
            P("groups", seq),
            P("groups"),
            P("groups"),
        ),
        out_specs=(P(every, None), P(every, None), P("groups", None)),
        check_vma=False,
    )
```

```python
import functools
import math

import jax
import jax.numpy as jnp
from jax import lax
from jax.experimental import pallas as pl
from jax.experimental.pallas import tpu as pltpu
from jax.sharding import Mesh, PartitionSpec as P

HEADS = 8
QK = 128
VDIM = 192
SPAN = 8
MIB = 1 << 20
VMEM = pl.BlockSpec(memory_space=pltpu.VMEM)
SMEM = pl.BlockSpec(memory_space=pltpu.SMEM)
HBM = pl.BlockSpec(memory_space=pltpu.HBM)


def chip_swap(cells, mask):
    count = lax.axis_size("chip")
    return lax.ppermute(cells, "chip", [(i, i ^ mask) for i in range(count)])


def core_swap(cells):
    return lax.ppermute(cells, "core", [(0, 1), (1, 0)])


def group_swap(cells):
    return lax.ppermute(cells, "groups", [(0, 1), (1, 0)])


def after(value, *others):
    return lax.optimization_barrier((value, *others))[0]


def bring(blocks, rows, extra, low, weight, tracks, sems):
    copies = []
    for at, block in enumerate(blocks):
        for which, (first, length, target) in enumerate(
            (
                (0, rows, weight.at[pl.ds(pl.multiple_of((low ^ at) * rows, 8), rows)]),
                (rows, extra, tracks.at[pl.ds(at * extra, extra)]),
            )
        ):
            copy = pltpu.make_async_copy(
                block.at[pl.ds(first, length)], target, sems.at[2 * at + which]
            )
            copy.start()
            copies.append(copy)
    return copies


def first_tokens_kernel(rows, extra, place_ref, own_hbm, partner_hbm, *refs):
    blocks, refs = refs[:-8], refs[-8:]
    total_ref, last_ref, tracks_ref, in_s, x_s, w_s, in_sems, block_sems = refs
    pair = x_s.shape[0]
    inputs = [
        pltpu.make_async_copy(ref, in_s.at[part], in_sems.at[part])
        for part, ref in enumerate((own_hbm, partner_hbm))
    ]
    for copy in inputs:
        copy.start()
    copies = [
        bring(
            blocks[4 * mask : 4 * mask + 4],
            rows,
            extra,
            place_ref[1],
            w_s.at[mask],
            tracks_ref.at[pl.ds(4 * mask * extra, 4 * extra)],
            block_sems.at[mask],
        )
        for mask in range(pair - 1)
    ]
    pairs, width = in_s.shape[1:]
    half = pairs // 2
    span = x_s.shape[2]
    line = lax.broadcasted_iota(jnp.int32, (half, pairs), 0)
    column = lax.broadcasted_iota(jnp.int32, (half, pairs), 1)
    for part, copy in enumerate(inputs):
        copy.wait()
        for tap in range(2):
            pick = (column == 2 * line + tap).astype(jnp.bfloat16)
            cells = jnp.dot(pick, in_s[part], preferred_element_type=jnp.float32).astype(
                jnp.bfloat16
            )
            for at in range(width // span):
                x_s[tap * (width // span) + at, part * half : (part + 1) * half, :] = cells[
                    :, at * span : (at + 1) * span
                ]
    total = jnp.zeros(total_ref.shape, jnp.float32)
    for mask in range(pair - 1):
        for copy in copies[mask]:
            copy.wait()
        total = total + jnp.dot(
            x_s[place_ref[0] ^ mask], w_s[mask], preferred_element_type=jnp.float32
        )
    total_ref[...] = total
    last_ref[...] = x_s[place_ref[0] ^ (pair - 1)]


def last_tokens_kernel(rows, extra, place_ref, total_ref, last_ref, *refs):
    blocks, (own_ref, partner_ref, tracks_ref, w_s, sems) = refs[:-5], refs[-5:]
    for copy in bring(blocks, rows, extra, place_ref[1], w_s, tracks_ref, sems):
        copy.wait()
    half = own_ref.shape[0]
    total = total_ref[...] + jnp.dot(last_ref[...], w_s[...], preferred_element_type=jnp.float32)
    own_ref[...] = total[:half].astype(jnp.bfloat16)
    partner_ref[...] = total[half:].astype(jnp.bfloat16)


def windows_kernel(grad_ref, out_ref):
    tracks = grad_ref.shape[0]
    count, lines, lanes = out_ref.shape
    rows = grad_ref.shape[1] // count
    lane = lax.broadcasted_iota(jnp.int32, (tracks, rows), 1)
    zero = jnp.zeros((tracks, rows), jnp.float32)
    out_ref[...] = jnp.zeros_like(out_ref)
    tiles = [grad_ref[:, at * rows : (at + 1) * rows].astype(jnp.float32) for at in range(count)]
    for at in range(count):
        after_it = tiles[at + 1] if at + 1 < count else zero
        before_it = pltpu.roll(tiles[at - 1], 2 * SPAN, 1) if at else zero
        edge = jnp.where(lane < SPAN, after_it, jnp.where(lane < 2 * SPAN, before_it, zero))
        out_ref[at, 0:tracks, 0:rows] = tiles[at].astype(out_ref.dtype)
        out_ref[at, 0:tracks, rows : 2 * rows] = edge.astype(out_ref.dtype)


def keyval_kernel(group_ref, mine_ref, theirs_ref, gain_ref, kv_ref, tok_ref, normed_ref, keyval_ref):
    width = mine_ref.shape[1]
    group = group_ref[0]
    tok_ref[:, pl.ds(pl.multiple_of(group * width, width), width)] = mine_ref[...]
    tok_ref[:, pl.ds(pl.multiple_of((1 - group) * width, width), width)] = theirs_ref[...]
    tok_f = tok_ref[...].astype(jnp.float32)
    inverse = lax.rsqrt(jnp.mean(tok_f * tok_f, axis=-1, keepdims=True) + 1e-06)
    normed = (tok_f * inverse * gain_ref[...]).astype(jnp.bfloat16)
    normed_ref[...] = normed
    keyval_ref[...] = lax.dot_general(
        normed, kv_ref[...], (((1,), (1,)), ((), ())), preferred_element_type=jnp.float32
    ).astype(jnp.bfloat16)


def sweep(turns, step, body, carry):
    if turns <= 4:
        for turn in range(turns):
            carry = body(turn * step, carry)
        return carry
    return lax.fori_loop(
        0, turns, lambda turn, held: body(pl.multiple_of(turn * step, step), held), carry
    )


def query_kernel(normed_ref, weight_ref, out_ref):
    rows = normed_ref.shape[0]
    query = jnp.dot(normed_ref[...], weight_ref[...], preferred_element_type=jnp.float32).astype(
        jnp.bfloat16
    )
    for h in range(HEADS):
        out_ref[h * rows : (h + 1) * rows, :] = query[:, h * QK : (h + 1) * QK]


def attention_kernel(row_block, key_block, pieces, first, last, query_ref, *refs):
    kv_refs, refs = refs[:pieces], refs[pieces:]
    if not first:
        old_top_ref, old_weighted_ref = refs[:2]
        refs = refs[2:]
    if last:
        tok_ref, outw_hbm, out_ref, k_s, v_s, s_s, context_s, outw_s, sem = refs
        token_rows = tok_ref.shape[0]
        fetch = pltpu.make_async_copy(outw_hbm, outw_s, sem)
        fetch.start()
    else:
        top_ref, weighted_ref, k_s, v_s, s_s = refs
    at = 0
    for ref in kv_refs:
        count = ref.shape[0]
        k_s[at : at + count, :] = ref[:, :QK]
        v_s[at : at + count, 0:VDIM] = ref[:, QK:]
        at += count
    key_block = min(key_block, at)
    v_s[:, VDIM:] = jnp.ones((at, v_s.shape[1] - VDIM), jnp.bfloat16)
    scale = QK ** (-0.5) / math.log(2.0)
    for r in range(0, query_ref.shape[0], row_block):
        rows = query_ref[r : r + row_block, :]
        slot = (r // row_block) % 2

        def score(k, top):
            scores = lax.dot_general(
                rows,
                k_s[pl.ds(k, key_block), :],
                (((1,), (1,)), ((), ())),
                preferred_element_type=jnp.float32,
            )
            s_s[slot, :, pl.ds(k, key_block)] = scores
            return jnp.maximum(top, jnp.max(scores, axis=1, keepdims=True))

        def weigh(k, weighted):
            shifted = s_s[slot, :, pl.ds(k, key_block)] - top
            expw = jnp.exp2(shifted * scale).astype(jnp.bfloat16)
            return weighted + jnp.dot(
                expw, v_s[pl.ds(k, key_block), :], preferred_element_type=jnp.float32
            )

        if first:
            old_top = jnp.full((row_block, 1), -jnp.inf, jnp.float32)
            start = jnp.zeros((row_block, v_s.shape[1]), jnp.float32)
        else:
            old_top = old_top_ref[r : r + row_block, 0:1]
        top = sweep(at // key_block, key_block, score, old_top)
        if not first:
            start = old_weighted_ref[r : r + row_block, :] * jnp.exp2((old_top - top) * scale)
        weighted = sweep(at // key_block, key_block, weigh, start)
        if last:
            context = (weighted[:, :VDIM] / weighted[:, VDIM : VDIM + 1]).astype(jnp.bfloat16)
            for j in range(row_block // token_rows):
                h = r // token_rows + j
                context_s[:, h * VDIM : (h + 1) * VDIM] = context[
                    j * token_rows : (j + 1) * token_rows
                ]
        else:
            top_ref[r : r + row_block, :] = jnp.broadcast_to(top, (row_block, top_ref.shape[1]))
            weighted_ref[r : r + row_block, :] = weighted
    if last:
        fetch.wait()
        added = jnp.dot(context_s[...], outw_s[...], preferred_element_type=jnp.float32)
        out_ref[...] = (tok_ref[...].astype(jnp.float32) + added).astype(jnp.bfloat16)


def decoder_kernel(extra, parts, tok_ref, grads_ref, taps_ref, *refs):
    chosen_refs, track_refs, (skip_ref, sums_ref) = refs[:parts], refs[parts:-2], refs[-2:]
    token_rows = tok_ref.shape[0]
    width = track_refs[0].shape[1]
    root = math.sqrt(2.0 / math.pi)
    masked = [
        lax.dot_general(
            grads_ref[...],
            chosen_ref[...],
            (((0,), (0,)), ((), ())),
            preferred_element_type=jnp.float32,
        )[: token_rows + 2 * SPAN]
        for chosen_ref in chosen_refs
    ]
    for side in range(2):
        at = side * width
        head = jnp.zeros((token_rows + 2 * SPAN, width), jnp.float32)
        for cells, tracks_ref in zip(masked, track_refs):
            column = lax.broadcasted_iota(jnp.int32, cells.shape, 1) % extra
            ours = (column < extra // 2) if side == 0 else (column >= extra // 2)
            rows = jnp.where(ours, cells, 0.0).astype(jnp.bfloat16)
            head = head + jnp.dot(rows, tracks_ref[...], preferred_element_type=jnp.float32)
        head = head.astype(jnp.bfloat16).astype(jnp.float32)
        own, later, earlier = (
            head[:token_rows],
            head[token_rows : token_rows + SPAN],
            head[token_rows + SPAN :],
        )
        shifted_rows = (
            jnp.concatenate([own[SPAN:], later], axis=0),
            own,
            jnp.concatenate([earlier, own[:-SPAN]], axis=0),
        )
        tok = tok_ref[:, at : at + width].astype(jnp.float32)
        square = tok * tok
        curve = jnp.tanh(root * (tok + 0.044715 * square * tok))
        gate = 0.5 * (1.0 + curve)
        act = tok * gate
        slope = gate + 0.5 * tok * (1.0 - curve * curve) * (root * (1.0 + 3 * 0.044715 * square))
        convback = jnp.zeros_like(tok)
        for tap, shifted in enumerate(shifted_rows):
            convback = convback + taps_ref[tap : tap + 1, at : at + width] * shifted
            sums_ref[tap : tap + 1, at : at + width] = jnp.sum(act * shifted, axis=0, keepdims=True)
        skip_ref[:, at : at + width] = (slope * convback).astype(jnp.bfloat16)


def call(body, out, specs, scratch=(), limit=32, name=None):
    return pl.pallas_call(
        body,
        out_shape=out,
        in_specs=specs,
        out_specs=jax.tree.map(lambda _: VMEM, out),
        scratch_shapes=list(scratch),
        compiler_params=pltpu.CompilerParams(vmem_limit_bytes=limit * MIB),
        name=name,
    )


def shards(
    enc_input,
    enc_weight,
    norm_gain,
    q_weight,
    kv_weight,
    out_weight,
    dec_weight,
    track_weight,
    track_grad,
    track_index,
    track_mask,
):
    chips = lax.axis_size("chip")
    count = 2 * chips
    pair = chips // 2
    token_rows = enc_input.shape[0] // 2
    rows, dim = enc_weight.shape
    width = dim // 2
    tracks = track_weight.shape[0]
    extra = 2 * tracks
    group = lax.axis_index("groups")
    me = lax.axis_index("chip") * 2 + lax.axis_index("core")
    shape = lambda *dims, kind=jnp.bfloat16: jax.ShapeDtypeStruct(dims, kind)
    direct = pair == 4 and rows % 16 == 0

    own_half = lax.dynamic_slice_in_dim(enc_weight, group * width, width, axis=1)
    packed = jnp.concatenate([own_half, track_weight[:, :width], track_weight[:, width:]], axis=0)
    partner_input = group_swap(enc_input)
    if direct:
        nears = [packed, chip_swap(packed, 2), chip_swap(packed, 4)]
        nears.append(chip_swap(after(packed, nears[1]), 6))
        crossed = [core_swap(near) for near in nears]
        fars = [chip_swap(near, 1) for near in nears]
        fars[1], fars[2] = (after(far, crossed[3]) for far in fars[1:3])
        blocks = [
            cells
            for near, other, far in zip(nears, crossed, fars)
            for cells in (near, other, far, core_swap(far))
        ]
        ids = me ^ jnp.arange(count, dtype=jnp.int32)
    else:
        ids = jnp.arange(count, dtype=jnp.int32)

    lines = -(-tracks // 16) * 16
    windows = call(
        windows_kernel, shape(count, lines, 2 * token_rows), [VMEM], limit=16, name="windows"
    )(track_grad.T)
    exchanged = lax.all_to_all(
        after(windows, crossed[0]) if direct else windows, ("chip", "core"), 0, 0, tiled=True
    )
    slots = jnp.pad(
        track_index.reshape(count, tracks), ((0, 0), (0, lines - tracks)), constant_values=-1
    )
    measured = jnp.pad(track_mask.reshape(count, tracks), ((0, 0), (0, lines - tracks)))
    column_tracks = ids[:, None] * tracks + jnp.arange(extra, dtype=jnp.int32)[None, :] % tracks
    chosen = [
        jnp.where(
            slots.reshape(-1, 1) == part.reshape(1, -1),
            measured.reshape(-1, 1).astype(jnp.bfloat16),
            0,
        ).astype(jnp.bfloat16)
        for part in ((column_tracks[:-4], column_tracks[-4:]) if direct else (column_tracks,))
    ]

    if direct:
        place = jnp.stack([lax.axis_index("chip") // 2, me % 4]).astype(jnp.int32)
        held = [pltpu.with_memory_space_constraint(block, pltpu.HBM) for block in blocks]
        span = 4 * rows
        total, last_cells, first_rows = call(
            functools.partial(first_tokens_kernel, rows, extra),
            (
                shape(2 * token_rows, width, kind=jnp.float32),
                shape(2 * token_rows, span),
                shape((count - 4) * extra, width),
            ),
            [SMEM] + [HBM] * (count - 2),
            scratch=(
                pltpu.VMEM((2,) + enc_input.shape, jnp.bfloat16),
                pltpu.VMEM((pair, 2 * token_rows, span), jnp.bfloat16),
                pltpu.VMEM((pair - 1, span, width), jnp.bfloat16),
                pltpu.SemaphoreType.DMA((2,)),
                pltpu.SemaphoreType.DMA((pair - 1, 8)),
            ),
            limit=16,
            name="first_tokens",
        )(
            place,
            *[
                pltpu.with_memory_space_constraint(cells, pltpu.HBM)
                for cells in (enc_input, partner_input)
            ],
            *held[:-4],
        )
        mine, partner, last_rows = call(
            functools.partial(last_tokens_kernel, rows, extra),
            (shape(token_rows, width), shape(token_rows, width), shape(4 * extra, width)),
            [SMEM] + [VMEM] * 2 + [HBM] * 4,
            scratch=(pltpu.VMEM((span, width), jnp.bfloat16), pltpu.SemaphoreType.DMA((8,))),
            limit=12,
            name="last_tokens",
        )(place, total, last_cells, *held[-4:])
        track_rows = [first_rows, last_rows]
    else:
        gathered = lax.all_gather(packed, ("chip", "core"), axis=0)
        track_rows = [gathered[:, rows:].reshape(count * extra, width)]
        weight = gathered[:, :rows].reshape(count * rows, width)
        mine, partner = (
            jnp.dot(
                cells.reshape(token_rows, count * rows), weight, preferred_element_type=jnp.float32
            ).astype(jnp.bfloat16)
            for cells in (enc_input, partner_input)
        )
    theirs = group_swap(partner)
    tokens, normed, keyval = call(
        keyval_kernel,
        (shape(token_rows, dim), shape(token_rows, dim), shape(token_rows, QK + VDIM)),
        [SMEM] + [VMEM] * 4,
        limit=8,
        name="keyval",
    )(group.reshape(1), mine, theirs, norm_gain.reshape(1, dim), kv_weight.T)

    if direct:
        nears = [chip_swap(keyval, 2 * mask) if mask else keyval for mask in range(pair)]
        fars = [chip_swap(near, 1) for near in nears]
        crossed = [core_swap(near) for near in nears]
        stages = [
            [
                cells
                for mask in masks
                for cells in (nears[mask], crossed[mask], fars[mask], core_swap(fars[mask]))
            ]
            for masks in ((0, 1), (2, 3))
        ]
    else:
        nears = crossed = [lax.all_gather(keyval, ("chip", "core"), axis=0, tiled=True)]
        stages = [nears]

    query = call(query_kernel, shape(HEADS * token_rows, QK), [VMEM] * 2, limit=8, name="query")(
        normed, q_weight
    )
    skip_grad, sums = call(
        functools.partial(decoder_kernel, extra, len(chosen)),
        (shape(token_rows, dim), shape(3, dim, kind=jnp.float32)),
        [VMEM] * (3 + 2 * len(chosen)),
        limit=16,
        name="decoder",
    )(
        after(tokens, nears[-1], query),
        exchanged.reshape(count * lines, 2 * token_rows),
        dec_weight,
        *chosen,
        *track_rows,
    )
    sums = sums + core_swap(sums)
    step = 1
    while step < chips:
        sums = sums + chip_swap(after(sums, crossed[-1]) if step == 2 else sums, step)
        step *= 2
    dec_weight_grad = sums / jnp.float32(math.sqrt(token_rows * count))

    row_block = 2 * token_rows if direct else token_rows
    state = []
    for turn, pieces in enumerate(stages):
        last = turn + 1 == len(stages)
        keys = sum(piece.shape[0] for piece in pieces)
        extras = (
            [tokens, pltpu.with_memory_space_constraint(out_weight, pltpu.HBM)] if last else []
        )
        held = (
            shape(token_rows, dim)
            if last
            else (
                shape(HEADS * token_rows, 128, kind=jnp.float32),
                shape(HEADS * token_rows, 256, kind=jnp.float32),
            )
        )
        state = call(
            functools.partial(attention_kernel, row_block, 512, len(pieces), turn == 0, last),
            held,
            [VMEM] * (1 + len(pieces) + len(state)) + ([VMEM, HBM] if last else []),
            scratch=(
                pltpu.VMEM((keys, QK), jnp.bfloat16),
                pltpu.VMEM((keys, 256), jnp.bfloat16),
                pltpu.VMEM((2, row_block, keys), jnp.float32),
            )
            + (
                (
                    pltpu.VMEM((token_rows, HEADS * VDIM), jnp.bfloat16),
                    pltpu.VMEM(out_weight.shape, jnp.bfloat16),
                    pltpu.SemaphoreType.DMA(()),
                )
                if last
                else ()
            ),
            limit=60 if len(stages) == 1 else 16,
            name="attention",
        )(query, *pieces, *state, *extras)
    return (state, skip_grad, dec_weight_grad)


def solution(mesh):
    groups, count = mesh.devices.shape
    inner = Mesh(mesh.devices.reshape(groups, count // 2, 2), ("groups", "chip", "core"))
    seq = ("chip", "core")
    every = ("groups", "chip", "core")
    return jax.shard_map(
        shards,
        mesh=inner,
        in_specs=(
            P(every, None),
            P(seq, None),
            P(),
            P(),
            P(),
            P(),
            P(),
            P(seq, None),
            P("groups", seq),
            P("groups"),
            P("groups"),
        ),
        out_specs=(P(every, None), P(every, None), P("groups", None)),
        check_vma=False,
    )
```

```python
import functools
import math

import jax
import jax.numpy as jnp
from jax import lax
from jax.experimental import pallas as pl
from jax.experimental.pallas import tpu as pltpu
from jax.sharding import Mesh, PartitionSpec as P

HEADS = 8
QK = 128
VDIM = 192
SPAN = 8
MIB = 1 << 20
COST = 1000
VMEM = pl.BlockSpec(memory_space=pltpu.VMEM)
SMEM = pl.BlockSpec(memory_space=pltpu.SMEM)
HBM = pl.BlockSpec(memory_space=pltpu.HBM)


def chip_swap(cells, mask):
    count = lax.axis_size("chip")
    return lax.ppermute(cells, "chip", [(i, i ^ mask) for i in range(count)])


def core_swap(cells):
    return lax.ppermute(cells, "core", [(0, 1), (1, 0)])


def group_swap(cells):
    return lax.ppermute(cells, "groups", [(0, 1), (1, 0)])


def after(value, *others):
    return lax.optimization_barrier((value, *others))[0]


def bring(same, cross, rows, extra, core, weight, tracks, sems):
    copies = []
    for at, block in enumerate((same, cross)):
        for which, (first, length, target) in enumerate(
            (
                (0, rows, weight.at[pl.ds(pl.multiple_of((core ^ at) * rows, 8), rows)]),
                (rows, extra, tracks.at[pl.ds(at * extra, extra)]),
            )
        ):
            copy = pltpu.make_async_copy(
                block.at[pl.ds(first, length)], target, sems.at[2 * at + which]
            )
            copy.start()
            copies.append(copy)
    return copies


def first_tokens_kernel(rows, extra, place_ref, own_hbm, partner_hbm, *refs):
    blocks, refs = refs[:-8], refs[-8:]
    total_ref, last_ref, tracks_ref, in_s, x_s, w_s, in_sems, block_sems = refs
    chips = x_s.shape[0]
    inputs = [
        pltpu.make_async_copy(ref, in_s.at[part], in_sems.at[part])
        for part, ref in enumerate((own_hbm, partner_hbm))
    ]
    for copy in inputs:
        copy.start()
    copies = [
        bring(
            blocks[2 * at],
            blocks[2 * at + 1],
            rows,
            extra,
            place_ref[1],
            w_s.at[at],
            tracks_ref.at[pl.ds(2 * at * extra, 2 * extra)],
            block_sems.at[at],
        )
        for at in range(chips - 1)
    ]
    pairs, width = in_s.shape[1:]
    half = pairs // 2
    span = x_s.shape[2]
    line = lax.broadcasted_iota(jnp.int32, (half, pairs), 0)
    column = lax.broadcasted_iota(jnp.int32, (half, pairs), 1)
    for part, copy in enumerate(inputs):
        copy.wait()
        for tap in range(2):
            pick = (column == 2 * line + tap).astype(jnp.bfloat16)
            cells = jnp.dot(pick, in_s[part], preferred_element_type=jnp.float32).astype(
                jnp.bfloat16
            )
            for at in range(width // span):
                x_s[tap * (width // span) + at, part * half : (part + 1) * half, :] = cells[
                    :, at * span : (at + 1) * span
                ]
    total = jnp.zeros(total_ref.shape, jnp.float32)
    for at in range(chips - 1):
        for copy in copies[at]:
            copy.wait()
        total = total + jnp.dot(
            x_s[place_ref[0] ^ at], w_s[at], preferred_element_type=jnp.float32
        )
    total_ref[...] = total
    last_ref[...] = x_s[place_ref[0] ^ (chips - 1)]


def last_tokens_kernel(rows, extra, place_ref, total_ref, last_ref, same, cross, *refs):
    own_ref, partner_ref, tracks_ref, w_s, sems = refs
    for copy in bring(same, cross, rows, extra, place_ref[1], w_s, tracks_ref, sems):
        copy.wait()
    half = own_ref.shape[0]
    total = total_ref[...] + jnp.dot(last_ref[...], w_s[...], preferred_element_type=jnp.float32)
    own_ref[...] = total[:half].astype(jnp.bfloat16)
    partner_ref[...] = total[half:].astype(jnp.bfloat16)


def windows_kernel(grad_ref, out_ref):
    tracks = grad_ref.shape[0]
    count, lines, lanes = out_ref.shape
    rows = grad_ref.shape[1] // count
    lane = lax.broadcasted_iota(jnp.int32, (tracks, rows), 1)
    zero = jnp.zeros((tracks, rows), jnp.float32)
    out_ref[...] = jnp.zeros_like(out_ref)
    tiles = [grad_ref[:, at * rows : (at + 1) * rows].astype(jnp.float32) for at in range(count)]
    for at in range(count):
        after_it = tiles[at + 1] if at + 1 < count else zero
        before_it = pltpu.roll(tiles[at - 1], 2 * SPAN, 1) if at else zero
        edge = jnp.where(lane < SPAN, after_it, jnp.where(lane < 2 * SPAN, before_it, zero))
        out_ref[at, 0:tracks, 0:rows] = tiles[at].astype(out_ref.dtype)
        out_ref[at, 0:tracks, rows : 2 * rows] = edge.astype(out_ref.dtype)


def skip_terms(tok, head, taps):
    token_rows = tok.shape[0]
    root = math.sqrt(2.0 / math.pi)
    own, later, earlier = (
        head[:token_rows],
        head[token_rows : token_rows + SPAN],
        head[token_rows + SPAN :],
    )
    square = tok * tok
    curve = jnp.tanh(root * (tok + 0.044715 * square * tok))
    gate = 0.5 * (1.0 + curve)
    act = tok * gate
    slope = gate + 0.5 * tok * (1.0 - curve * curve) * (root * (1.0 + 3 * 0.044715 * square))
    convback = jnp.zeros_like(tok)
    sums = []
    for tap, shifted in enumerate(
        (
            jnp.concatenate([own[SPAN:], later], axis=0),
            own,
            jnp.concatenate([earlier, own[:-SPAN]], axis=0),
        )
    ):
        convback = convback + taps[tap : tap + 1] * shifted
        sums.append(jnp.sum(act * shifted, axis=0, keepdims=True))
    return (slope * convback).astype(jnp.bfloat16), sums


def decoder_kernel(extra, parts, group_ref, mine_ref, grads_ref, taps_ref, *refs):
    chosen_refs, track_refs, (skip_ref, sums_ref, head_ref) = (
        refs[:parts],
        refs[parts:-3],
        refs[-3:],
    )
    group = group_ref[0]
    token_rows, width = mine_ref.shape
    masked = [
        lax.dot_general(
            grads_ref[...],
            chosen_ref[...],
            (((0,), (0,)), ((), ())),
            preferred_element_type=jnp.float32,
        )[: token_rows + 2 * SPAN]
        for chosen_ref in chosen_refs
    ]
    heads = []
    for side in (group, 1 - group):
        head = jnp.zeros((token_rows + 2 * SPAN, width), jnp.float32)
        for cells, tracks_ref in zip(masked, track_refs):
            column = lax.broadcasted_iota(jnp.int32, cells.shape, 1) % extra // (extra // 2)
            rows = jnp.where(column == side, cells, 0.0).astype(jnp.bfloat16)
            head = head + jnp.dot(rows, tracks_ref[...], preferred_element_type=jnp.float32)
        heads.append(head.astype(jnp.bfloat16))
    head_ref[...] = heads[1]
    taps = taps_ref[:, pl.ds(pl.multiple_of(group * width, width), width)]
    skip, sums = skip_terms(mine_ref[...].astype(jnp.float32), heads[0].astype(jnp.float32), taps)
    skip_ref[...] = skip
    for tap, term in enumerate(sums):
        sums_ref[tap : tap + 1, :] = term


def keyval_kernel(
    group_ref,
    mine_ref,
    skip_mine_ref,
    sums_mine_ref,
    head_ref,
    taps_ref,
    gain_ref,
    kv_ref,
    theirs_ref,
    tok_ref,
    normed_ref,
    block_ref,
    skip_ref,
    sums_s,
):
    token_rows, width = mine_ref.shape
    group = group_ref[0]
    here = pl.ds(pl.multiple_of(group * width, width), width)
    there = pl.ds(pl.multiple_of((1 - group) * width, width), width)
    tok_ref[:, here] = mine_ref[...]
    tok_ref[:, there] = theirs_ref[...]
    tok_f = tok_ref[...].astype(jnp.float32)
    inverse = lax.rsqrt(jnp.mean(tok_f * tok_f, axis=-1, keepdims=True) + 1e-06)
    normed = (tok_f * inverse * gain_ref[...]).astype(jnp.bfloat16)
    normed_ref[...] = normed
    block_ref[0:token_rows, 0 : QK + VDIM] = lax.dot_general(
        normed, kv_ref[...], (((1,), (1,)), ((), ())), preferred_element_type=jnp.float32
    ).astype(jnp.bfloat16)
    block_ref[0:token_rows, QK + VDIM :] = jnp.zeros(
        (token_rows, block_ref.shape[1] - QK - VDIM), jnp.bfloat16
    )
    skip, sums = skip_terms(
        theirs_ref[...].astype(jnp.float32), head_ref[...].astype(jnp.float32), taps_ref[:, there]
    )
    skip_ref[:, here] = skip_mine_ref[...]
    skip_ref[:, there] = skip
    sums_s[0:3, here] = sums_mine_ref[...]
    for tap, term in enumerate(sums):
        sums_s[tap : tap + 1, there] = term
    lanes = block_ref.shape[1]
    rows = [
        sums_s[tap : tap + 1, at : at + lanes]
        for tap in range(3)
        for at in range(0, 2 * width, lanes)
    ]
    exact = jnp.concatenate(rows, axis=0)
    coarse = exact.astype(jnp.bfloat16).astype(jnp.float32)
    block_ref[token_rows:, :] = jnp.concatenate([coarse, exact - coarse], axis=0).astype(
        jnp.bfloat16
    )


def add_terms(blocks):
    if len(blocks) == 1:
        rows = blocks[0].astype(jnp.float32)
        return rows[: rows.shape[0] // 2] + rows[rows.shape[0] // 2 :]
    half = len(blocks) // 2
    return add_terms(blocks[:half]) + add_terms(blocks[half:])


def sweep(turns, step, body, carry):
    if turns <= 4:
        for turn in range(turns):
            carry = body(turn * step, carry)
        return carry
    return lax.fori_loop(
        0, turns, lambda turn, held: body(pl.multiple_of(turn * step, step), held), carry
    )


def query_kernel(normed_ref, weight_ref, out_ref):
    rows = normed_ref.shape[0]
    query = jnp.dot(normed_ref[...], weight_ref[...], preferred_element_type=jnp.float32).astype(
        jnp.bfloat16
    )
    for h in range(HEADS):
        out_ref[h * rows : (h + 1) * rows, :] = query[:, h * QK : (h + 1) * QK]


def attention_kernel(row_block, key_block, tokens_each, pieces, first, last, query_ref, *refs):
    kv_refs, refs = refs[:pieces], refs[pieces:]
    riders = kv_refs[0].shape[0] > tokens_each
    if not first:
        old_top_ref, old_weighted_ref, old_terms_ref = refs[:3]
        refs = refs[3:]
    if last:
        tok_ref, outw_hbm, out_ref = refs[:3]
        refs = refs[3:]
        if riders:
            sums_ref, refs = refs[0], refs[1:]
        k_s, v_s, s_s, context_s, outw_s, sem = refs
        token_rows = tok_ref.shape[0]
        fetch = pltpu.make_async_copy(outw_hbm, outw_s, sem)
        fetch.start()
    else:
        top_ref, weighted_ref, terms_ref, k_s, v_s, s_s = refs
    at = 0
    for ref in kv_refs:
        k_s[at : at + tokens_each, :] = ref[0:tokens_each, :QK]
        v_s[at : at + tokens_each, 0:VDIM] = ref[0:tokens_each, QK : QK + VDIM]
        at += tokens_each
    key_block = min(key_block, at)
    v_s[:, VDIM:] = jnp.ones((at, v_s.shape[1] - VDIM), jnp.bfloat16)
    if riders:
        terms = add_terms([ref[tokens_each:, :] for ref in kv_refs])
        if not first:
            terms = terms + old_terms_ref[...]
        if last:
            terms = terms * ((2 * pieces * tokens_each) ** (-0.5))
            lanes = terms.shape[1]
            turns = sums_ref.shape[1] // lanes
            for row in range(terms.shape[0]):
                tap, spot = row // turns, row % turns * lanes
                sums_ref[tap : tap + 1, spot : spot + lanes] = terms[row : row + 1, :]
        else:
            terms_ref[...] = terms
    scale = QK ** (-0.5) / math.log(2.0)
    for r in range(0, query_ref.shape[0], row_block):
        rows = query_ref[r : r + row_block, :]
        slot = (r // row_block) % 2

        def score(k, top):
            scores = lax.dot_general(
                rows,
                k_s[pl.ds(k, key_block), :],
                (((1,), (1,)), ((), ())),
                preferred_element_type=jnp.float32,
            )
            s_s[slot, :, pl.ds(k, key_block)] = scores
            return jnp.maximum(top, jnp.max(scores, axis=1, keepdims=True))

        def weigh(k, weighted):
            shifted = s_s[slot, :, pl.ds(k, key_block)] - top
            expw = jnp.exp2(shifted * scale).astype(jnp.bfloat16)
            return weighted + jnp.dot(
                expw, v_s[pl.ds(k, key_block), :], preferred_element_type=jnp.float32
            )

        if first:
            old_top = jnp.full((row_block, 1), -jnp.inf, jnp.float32)
            start = jnp.zeros((row_block, v_s.shape[1]), jnp.float32)
        else:
            old_top = old_top_ref[r : r + row_block, 0:1]
        top = sweep(at // key_block, key_block, score, old_top)
        if not first:
            start = old_weighted_ref[r : r + row_block, :] * jnp.exp2((old_top - top) * scale)
        weighted = sweep(at // key_block, key_block, weigh, start)
        if last:
            context = (weighted[:, :VDIM] / weighted[:, VDIM : VDIM + 1]).astype(jnp.bfloat16)
            for j in range(row_block // token_rows):
                h = r // token_rows + j
                context_s[:, h * VDIM : (h + 1) * VDIM] = context[
                    j * token_rows : (j + 1) * token_rows
                ]
        else:
            top_ref[r : r + row_block, :] = jnp.broadcast_to(top, (row_block, top_ref.shape[1]))
            weighted_ref[r : r + row_block, :] = weighted
    if last:
        fetch.wait()
        added = jnp.dot(context_s[...], outw_s[...], preferred_element_type=jnp.float32)
        out_ref[...] = (tok_ref[...].astype(jnp.float32) + added).astype(jnp.bfloat16)


def call(body, out, specs, scratch=(), limit=32, name=None, us=1):
    return pl.pallas_call(
        body,
        out_shape=out,
        in_specs=specs,
        out_specs=jax.tree.map(lambda _: VMEM, out),
        scratch_shapes=list(scratch),
        compiler_params=pltpu.CompilerParams(vmem_limit_bytes=limit * MIB),
        cost_estimate=pl.CostEstimate(
            flops=int(us * COST), transcendentals=0, bytes_accessed=int(us * 1e3)
        ),
        name=name,
    )


def shards(
    enc_input,
    enc_weight,
    norm_gain,
    q_weight,
    kv_weight,
    out_weight,
    dec_weight,
    track_weight,
    track_grad,
    track_index,
    track_mask,
):
    chips = lax.axis_size("chip")
    count = 2 * chips
    pair = chips // 2
    token_rows = enc_input.shape[0] // 2
    rows, dim = enc_weight.shape
    width = dim // 2
    tracks = track_weight.shape[0]
    extra = 2 * tracks
    group = lax.axis_index("groups")
    me = lax.axis_index("chip") * 2 + lax.axis_index("core")
    shape = lambda *dims, kind=jnp.bfloat16: jax.ShapeDtypeStruct(dims, kind)
    direct = pair == 4 and rows % 16 == 0

    own_half = lax.dynamic_slice_in_dim(enc_weight, group * width, width, axis=1)
    packed = jnp.concatenate([own_half, track_weight[:, :width], track_weight[:, width:]], axis=0)
    partner_input = group_swap(enc_input)
    if direct:
        nears = [packed] + [chip_swap(packed, 2 * mask) for mask in range(1, pair)]
        same = [cells for near in nears for cells in (near, chip_swap(near, 1))]
        blocks = [cells for part in same[:-1] for cells in (part, core_swap(part))]
        ids = me ^ jnp.arange(count, dtype=jnp.int32)
    else:
        ids = jnp.arange(count, dtype=jnp.int32)

    lines = -(-tracks // 16) * 16
    windows = call(
        windows_kernel, shape(count, lines, 2 * token_rows), [VMEM], limit=16, name="windows"
    )(track_grad.T)
    slots = jnp.pad(
        track_index.reshape(count, tracks), ((0, 0), (0, lines - tracks)), constant_values=-1
    )
    measured = jnp.pad(track_mask.reshape(count, tracks), ((0, 0), (0, lines - tracks)))
    column_tracks = ids[:, None] * tracks + jnp.arange(extra, dtype=jnp.int32)[None, :] % tracks
    chosen = [
        jnp.where(
            slots.reshape(-1, 1) == part.reshape(1, -1),
            measured.reshape(-1, 1).astype(jnp.bfloat16),
            0,
        ).astype(jnp.bfloat16)
        for part in ((column_tracks[:-2], column_tracks[-2:]) if direct else (column_tracks,))
    ]

    if direct:
        place = jnp.stack([lax.axis_index("chip"), lax.axis_index("core")]).astype(jnp.int32)
        here = lambda *cells: [pltpu.with_memory_space_constraint(c, pltpu.HBM) for c in cells]
        span = 2 * rows
        total, last_cells, first_rows = call(
            functools.partial(first_tokens_kernel, rows, extra),
            (
                shape(2 * token_rows, width, kind=jnp.float32),
                shape(2 * token_rows, span),
                shape((count - 2) * extra, width),
            ),
            [SMEM] + [HBM] * count,
            scratch=(
                pltpu.VMEM((2,) + enc_input.shape, jnp.bfloat16),
                pltpu.VMEM((chips, 2 * token_rows, span), jnp.bfloat16),
                pltpu.VMEM((chips - 1, span, width), jnp.bfloat16),
                pltpu.SemaphoreType.DMA((2,)),
                pltpu.SemaphoreType.DMA((chips - 1, 4)),
            ),
            limit=16,
            name="first_tokens",
            us=5,
        )(place, *here(enc_input, partner_input, *blocks))
        final, total = lax.optimization_barrier((same[-1], total))
        mine, partner, last_rows = call(
            functools.partial(last_tokens_kernel, rows, extra),
            (shape(token_rows, width), shape(token_rows, width), shape(2 * extra, width)),
            [SMEM] + [VMEM] * 2 + [HBM] * 2,
            scratch=(pltpu.VMEM((span, width), jnp.bfloat16), pltpu.SemaphoreType.DMA((4,))),
            limit=12,
            name="last_tokens",
            us=2,
        )(place, total, last_cells, *here(final, core_swap(final)))
        track_rows = [first_rows, last_rows]
    else:
        gathered = lax.all_gather(packed, ("chip", "core"), axis=0)
        track_rows = [gathered[:, rows:].reshape(count * extra, width)]
        weight = gathered[:, :rows].reshape(count * rows, width)
        mine, partner = (
            jnp.dot(
                cells.reshape(token_rows, count * rows), weight, preferred_element_type=jnp.float32
            ).astype(jnp.bfloat16)
            for cells in (enc_input, partner_input)
        )
    theirs = group_swap(partner)
    exchanged = lax.all_to_all(after(windows, partner), ("chip", "core"), 0, 0, tiled=True)
    skip_mine, sums_mine, head = call(
        functools.partial(decoder_kernel, extra, len(chosen)),
        (
            shape(token_rows, width),
            shape(3, width, kind=jnp.float32),
            shape(token_rows + 2 * SPAN, width),
        ),
        [SMEM] + [VMEM] * (3 + 2 * len(chosen)),
        limit=16,
        name="decoder",
        us=2,
    )(
        group.reshape(1),
        mine,
        exchanged.reshape(count * lines, 2 * token_rows),
        dec_weight,
        *chosen,
        *track_rows,
    )
    lanes = 384
    terms = 3 * dim // lanes
    tokens, normed, block, skip_grad = call(
        keyval_kernel,
        (
            shape(token_rows, dim),
            shape(token_rows, dim),
            shape(token_rows + 2 * terms, lanes),
            shape(token_rows, dim),
        ),
        [SMEM] + [VMEM] * 8,
        scratch=(pltpu.VMEM((8, dim), jnp.float32),),
        limit=12,
        name="keyval",
        us=2,
    )(
        group.reshape(1),
        mine,
        skip_mine,
        sums_mine,
        head,
        dec_weight,
        norm_gain.reshape(1, dim),
        kv_weight.T,
        theirs,
    )

    if direct:
        nears = [chip_swap(block, 2 * mask) if mask else block for mask in range(pair)]
        fars = [chip_swap(near, 1) for near in nears]
        stages = [
            [
                cells
                for mask in masks
                for cells in (nears[mask], core_swap(nears[mask]), fars[mask], core_swap(fars[mask]))
            ]
            for masks in ((0, 1), (2, 3))
        ]
        each = token_rows
    else:
        gathered = lax.all_gather(block, ("chip", "core"), axis=0)
        stages = [[gathered[:, :token_rows].reshape(count * token_rows, lanes)]]
        each = count * token_rows
        sums = jnp.sum(
            gathered[:, token_rows:].astype(jnp.float32).reshape(2 * count, terms, lanes), axis=0
        )
        dec_weight_grad = sums.reshape(3, dim) / jnp.float32(math.sqrt(token_rows * count))

    query = call(query_kernel, shape(HEADS * token_rows, QK), [VMEM] * 2, limit=8, name="query")(
        normed, q_weight
    )
    row_block = 2 * token_rows if direct else token_rows
    state = []
    for turn, pieces in enumerate(stages):
        last = turn + 1 == len(stages)
        keys = len(pieces) * each
        extras = (
            [tokens, pltpu.with_memory_space_constraint(out_weight, pltpu.HBM)] if last else []
        )
        if last:
            held = (shape(token_rows, dim),) + (
                (shape(3, dim, kind=jnp.float32),) if direct else ()
            )
        else:
            held = (
                shape(HEADS * token_rows, 128, kind=jnp.float32),
                shape(HEADS * token_rows, 256, kind=jnp.float32),
                shape(terms, lanes, kind=jnp.float32),
            )
        state = call(
            functools.partial(
                attention_kernel, row_block, 512, each, len(pieces), turn == 0, last
            ),
            held,
            [VMEM] * (1 + len(pieces) + len(state)) + ([VMEM, HBM] if last else []),
            scratch=(
                pltpu.VMEM((keys, QK), jnp.bfloat16),
                pltpu.VMEM((keys, 256), jnp.bfloat16),
                pltpu.VMEM((2, row_block, keys), jnp.float32),
            )
            + (
                (
                    pltpu.VMEM((token_rows, HEADS * VDIM), jnp.bfloat16),
                    pltpu.VMEM(out_weight.shape, jnp.bfloat16),
                    pltpu.SemaphoreType.DMA(()),
                )
                if last
                else ()
            ),
            limit=60 if len(stages) == 1 else 16,
            name="attention",
            us=5 if last else 2,
        )(query, *pieces, *state, *extras)
    if direct:
        return (state[0], skip_grad, state[1])
    return (state[0], skip_grad, dec_weight_grad)


def solution(mesh):
    groups, count = mesh.devices.shape
    inner = Mesh(mesh.devices.reshape(groups, count // 2, 2), ("groups", "chip", "core"))
    seq = ("chip", "core")
    every = ("groups", "chip", "core")
    return jax.shard_map(
        shards,
        mesh=inner,
        in_specs=(
            P(every, None),
            P(seq, None),
            P(),
            P(),
            P(),
            P(),
            P(),
            P(seq, None),
            P("groups", seq),
            P("groups"),
            P("groups"),
        ),
        out_specs=(P(every, None), P(every, None), P("groups", None)),
        check_vma=False,
    )
```
